256 devices in a mesh: energy: 4 (over z_lo), cluster: 16 (over x, y), tile: 4 (over z_hi, core).
Axes of the slice: x: 4, y: 4, z: 8 (z_hi: 2, z_lo: 4; z = z_hi * 4 + z_lo), core: 2. Of those that a mesh axis runs over, the one named last changes fastest.
Arguments:
- boundary: bfloat16 [16, 2, 512, 8, 2, 1024], P('cluster', None, 'tile', 'energy'), may hold values from -5 to 5
- column_source: int32 [16, 1024], P('cluster'), may hold values from 0 to 1023, as said below
- energy_weights: float32 [8], P('energy'), may hold values from 0.2 to 2
Outputs:
- final_rows: float32 [16, 256, 8, 2, 1024], P('cluster', 'tile', 'energy')
- density: float32 [16, 256], P('cluster', 'tile')
The draws below stay inside these ranges and needn't reach their ends.
Inputs may be any that keep to these rules, and one draw needn't show every extreme that they name: `column_source`: for each cluster, every index 0 to 1023 appears once.
All inputs are finite; a program needn't handle non-finite values.
Results may differ from the reference program's by a relative error of at most 0.015.
Values may be sent and summed in bfloat16 or wider, within the bound.
No kernel may reach another device: no remote copies, remote signals or barrier semaphores. Data moves between devices by JAX's collectives and lax.ppermute only.
A program may use at most 64 MiB of HBM per device.

```python
import math
import jax
import jax.numpy as jnp
from jax import lax

S = 512
B = 1024
NE = 8
NC = 16
LEVELS = 2
ROWS = 128
OUT_ROWS = 256


def shared_order(key):
    keys = jax.random.split(jax.random.fold_in(key, 11), NC)
    return jax.vmap(lambda single_key: jax.random.permutation(single_key, B))(keys).astype(jnp.int32)


def draw_column_source(key, part):
    return shared_order(key)


def draw_boundary(key, part):
    order = shared_order(key)
    shape = (NC, 2, S, NE, 2, B)
    keys = jax.random.split(jax.random.fold_in(key, 23), 3)
    couple_scale = 0.9 * S ** (-0.25)
    node_of_column = jax.vmap(lambda single_order: jnp.zeros((B,), jnp.int32).at[single_order].set(jnp.arange(B, dtype=jnp.int32)))(order)
    column_outer = (node_of_column >= S)[:, None, None, None, None, :]
    row_outer = (jnp.arange(2) == 1)[None, :, None, None, None, None]
    coupled = column_outer != row_outer
    base = jax.random.truncated_normal(keys[0], -3.0, 3.0, shape, jnp.float32)
    diag_real = jax.random.uniform(keys[1], (NC, 2, S, NE), jnp.float32, 2.0, 4.0)
    diag_imag = jax.random.uniform(keys[2], (NC, 2, S, NE), jnp.float32, 0.2, 1.0)
    noise = base * jnp.where(coupled, couple_scale, 0.04)
    target = order.reshape(NC, 2, S)
    hitting = (jnp.arange(B)[None, None, None, :] == target[:, :, :, None])[:, :, :, None, None, :]
    diagonal = jnp.stack([diag_real, diag_imag], axis=4)[..., None]
    return (noise + jnp.where(hitting, diagonal, 0.0)).astype(jnp.bfloat16)


def level_of(rng, shape, cuts, smallest, largest):
    gain = 1.0
    for axis_at, shards_of in cuts:
        heights = jax.random.uniform(jax.random.fold_in(jax.random.fold_in(rng, 6), axis_at), (shards_of,), jnp.float32, smallest / len(cuts), largest / len(cuts))
        gain = gain * jnp.repeat(jnp.exp(heights), shape[axis_at] // shards_of).reshape((-1,) + (1,) * (len(shape) - 1 - axis_at))
    return gain


def setup_inputs(seed: int = 0) -> dict:
    streams_of = jax.random.split(jax.random.key(seed), 4)
    boundary = draw_boundary(jax.random.fold_in(streams_of[3], 71), 0)
    column_source = draw_column_source(jax.random.fold_in(streams_of[3], 71), 0)
    energy_weights = jnp.clip(jnp.exp(math.log(2.0) - 2.3025851 * jax.random.uniform(streams_of[2], (NE,), jnp.float32) ** level_of(streams_of[2], (NE,), ((0, 4),), -0.2, 0.2)), 0.2, 2.0)
    return dict(boundary=boundary, column_source=column_source, energy_weights=energy_weights)


def complex_dot(left, right):
    real_part = jnp.dot(left[0], right[0], preferred_element_type=jnp.float32) - jnp.dot(left[1], right[1], preferred_element_type=jnp.float32)
    imag_part = jnp.dot(left[0], right[1], preferred_element_type=jnp.float32) + jnp.dot(left[1], right[0], preferred_element_type=jnp.float32)
    return jnp.stack([real_part, imag_part])


def inverse_guess(interior):
    values = interior.astype(jnp.float32)
    diag_real = jnp.diagonal(values[0])
    diag_imag = jnp.diagonal(values[1])
    denom = diag_real * diag_real + diag_imag * diag_imag
    inv_real = diag_real / denom
    inv_imag = -diag_imag / denom
    temp_real = values[0] * inv_real[None, :] - values[1] * inv_imag[None, :]
    temp_imag = values[0] * inv_imag[None, :] + values[1] * inv_real[None, :]
    prod_real = inv_real[:, None] * temp_real - inv_imag[:, None] * temp_imag
    prod_imag = inv_real[:, None] * temp_imag + inv_imag[:, None] * temp_real
    ident = jnp.eye(values.shape[1], dtype=jnp.float32)
    guess_real = 2.0 * ident * inv_real[:, None] - prod_real
    guess_imag = 2.0 * ident * inv_imag[:, None] - prod_imag
    return jnp.stack([guess_real, guess_imag]).astype(jnp.bfloat16)


def merge_pair(low, high):
    interior = (low[:, :S, :S] + high[:, :S, :S]).astype(jnp.bfloat16)
    approx_inverse = inverse_guess(interior)
    left = jnp.concatenate([low[:, S:, :S], high[:, S:, :S]], axis=1).astype(jnp.bfloat16)
    right = jnp.concatenate([low[:, :S, S:], high[:, :S, S:]], axis=2).astype(jnp.bfloat16)
    applied = complex_dot(left, approx_inverse)
    middle = complex_dot(applied.astype(jnp.bfloat16), interior).astype(jnp.bfloat16)
    reduced = (2.0 * applied - complex_dot(middle, approx_inverse)).astype(jnp.bfloat16)
    zeros = jnp.zeros_like(low[:, S:, S:])
    upper = jnp.concatenate([low[:, S:, S:], zeros], axis=2)
    lower = jnp.concatenate([zeros, high[:, S:, S:]], axis=2)
    start = jnp.concatenate([upper, lower], axis=1)
    return start - complex_dot(reduced, right)


def reference(boundary, column_source, energy_weights):
    clusters = jnp.arange(NC).astype(jnp.int32)
    group = clusters // (2 ** LEVELS)
    side_bit = (clusters // (2 ** (LEVELS - 1))) % 2
    within = clusters % (2 ** (LEVELS - 1))
    quarter = ROWS // (2 ** (LEVELS - 1))
    index = jnp.arange(OUT_ROWS).astype(jnp.int32)
    rows = side_bit[:, None] * S + (index[None, :] // quarter) * ROWS + within[:, None] * quarter + index[None, :] % quarter

    def energy_step(energy):
        stored = lax.dynamic_index_in_dim(boundary, energy, 3, keepdims=False)
        canonical = jnp.take_along_axis(stored, column_source[:, None, None, None, :], axis=4)
        blocks = canonical.reshape(NC, B, 2, B).transpose(0, 2, 1, 3).astype(jnp.float32)
        for level_index in range(LEVELS):
            paired = blocks.reshape(-1, 2, 2, B, B)
            blocks = jax.vmap(merge_pair)(paired[:, 0], paired[:, 1])
        picked = blocks[group[:, None], :, rows, :]
        diagonal = blocks[group[:, None], 1, rows, rows]
        return picked, diagonal

    picked, diagonal = lax.map(energy_step, jnp.arange(NE).astype(jnp.int32))
    final_rows = picked.transpose(1, 2, 0, 3, 4)
    density = jnp.sum(energy_weights[:, None, None] * diagonal, axis=0)
    return final_rows, density
```

```python
import jax
import jax.numpy as jnp
from jax import lax
from jax.experimental import pallas as pl
from jax.experimental.pallas import tpu as pltpu
from jax.sharding import PartitionSpec as P


F32 = jnp.float32
BF16 = jnp.bfloat16


def exchange(x, axis, distance):
    return lax.ppermute(x, axis, [(i, i ^ distance) for i in range(lax.axis_size(axis))])


def dot(x, y):
    return jnp.dot(x, y, preferred_element_type=F32)


def product(x, y):
    real = dot(x[0], y[0]) - dot(x[1], y[1])
    imag = dot(x[0], y[1]) + dot(x[1], y[0])
    return real, imag


def halved(pair):
    return pair[0].astype(BF16), pair[1].astype(BF16)


def guess(interior, approx):
    size = interior.shape[1]
    real = interior[0].astype(F32)
    imag = interior[1].astype(F32)
    on_diag = lax.broadcasted_iota(jnp.int32, (size, size), 0) == lax.broadcasted_iota(
        jnp.int32, (size, size), 1
    )
    masked_real = jnp.where(on_diag, real, 0.0)
    masked_imag = jnp.where(on_diag, imag, 0.0)

    def reciprocal(axis):
        diag_real = jnp.sum(masked_real, axis=axis, keepdims=True)
        diag_imag = jnp.sum(masked_imag, axis=axis, keepdims=True)
        denom = diag_real * diag_real + diag_imag * diag_imag
        return diag_real / denom, -diag_imag / denom

    col_real, col_imag = reciprocal(0)
    row_real, row_imag = reciprocal(1)
    temp_real = real * col_real - imag * col_imag
    temp_imag = real * col_imag + imag * col_real
    prod_real = row_real * temp_real - row_imag * temp_imag
    prod_imag = row_real * temp_imag + row_imag * temp_real
    approx[0] = (jnp.where(on_diag, 2.0 * row_real, 0.0) - prod_real).astype(BF16)
    approx[1] = (jnp.where(on_diag, 2.0 * row_imag, 0.0) - prod_imag).astype(BF16)


def eliminate(left, interior, approx):
    inverse = (approx[0], approx[1])
    applied = product(left, inverse)
    middle = halved(product(halved(applied), (interior[0], interior[1])))
    second = product(middle, inverse)
    return halved((2.0 * applied[0] - second[0], 2.0 * applied[1] - second[1]))


def whole(array):
    return pl.BlockSpec(memory_space=pltpu.VMEM)


def first_level(half):
    width = half

    def body(where_ref, *refs):
        sep = refs[:8]
        outer = refs[8:12]
        sep_out, rest_out = refs[12:14]
        interior, approx, right, left, start = refs[14:]
        side, depth, core = where_ref[0], where_ref[1], where_ref[2]
        rows = sep[0].shape[1]
        for core_step in range(2):
            for depth_step in range(2):
                own = sep[core_step * 4 + depth_step * 2]
                other = sep[core_step * 4 + depth_step * 2 + 1]
                tile = (depth ^ depth_step) * 2 + (core ^ core_step)
                at = pl.ds(pl.multiple_of(tile * rows, rows), rows)
                own_at = pl.multiple_of(side * width, width)
                other_at = pl.multiple_of((1 - side) * width, width)
                for part in range(2):
                    interior[part, at, :] = (
                        own[part, :, :width].astype(F32) + other[part, :, :width].astype(F32)
                    ).astype(BF16)
                    right[part, at, pl.ds(own_at, width)] = own[part, :, width:]
                    right[part, at, pl.ds(other_at, width)] = other[part, :, width:]
        guess(interior, approx)
        few = outer[0].shape[1]
        for depth_step in range(2):
            for turn in range(2):
                piece = outer[depth_step * 2 + turn]
                at = (side ^ turn) * (2 * few) + (depth ^ depth_step) * few
                at = pl.ds(pl.multiple_of(at, few), few)
                for part in range(2):
                    left[part, at, :] = piece[part, :, :width]
                    start[part, at, :] = piece[part, :, width:]
        reduced = eliminate((left[0], left[1]), interior, approx)
        taken = product(reduced, (right[0], right[1]))
        count = 2 * few
        for part in range(2):
            block = taken[part]
            sep_out[part, :, :width] = (
                start[part, :count].astype(F32) - block[:count, :width]
            ).astype(BF16)
            sep_out[part, :, width:] = (-block[:count, width:]).astype(BF16)
            rest_out[part, :, :width] = -block[count:, :width]
            rest_out[part, :, width:] = start[part, count:].astype(F32) - block[count:, width:]

    return body


def last_level(half):
    width = half

    def body(where_ref, *refs):
        sep = refs[:8]
        rest, row_at = refs[8:10]
        keep_out, send_out, diag_out = refs[10:13]
        interior, approx, right, total = refs[13:]
        side, depth, core, pair = where_ref[0], where_ref[1], where_ref[2], where_ref[3]
        count = sep[0].shape[1]
        few = count // 2
        for core_step in range(2):
            for side_step in range(2):
                own = sep[core_step * 4 + side_step]
                other = sep[core_step * 4 + 2 + side_step]
                own_at = pl.multiple_of(pair * width, width)
                other_at = pl.multiple_of((1 - pair) * width, width)
                for deep in range(2):
                    src = pl.ds(deep * few, few)
                    at = (deep * 2 + (core ^ core_step)) * count + (side ^ side_step) * few
                    at = pl.ds(pl.multiple_of(at, few), few)
                    for part in range(2):
                        interior[part, at, :] = (
                            own[part, src, :width].astype(F32) + other[part, src, :width].astype(F32)
                        ).astype(BF16)
                        right[part, at, pl.ds(own_at, width)] = own[part, src, width:]
                        right[part, at, pl.ds(other_at, width)] = other[part, src, width:]
        guess(interior, approx)
        left = (rest[0, :, :width].astype(BF16), rest[1, :, :width].astype(BF16))
        reduced = eliminate(left, interior, approx)
        taken = product(reduced, (right[0], right[1]))
        for part in range(2):
            total[part] = -taken[part]
            at = pl.ds(pl.multiple_of(pair * width, width), width)
            total[part, :, at] = total[part, :, at] + rest[part, :, width:]
        columns = lax.broadcasted_iota(jnp.int32, (count, 2 * width), 1)
        picked = jnp.where(columns == row_at[...], total[1], 0.0)
        diag_out[...] = jnp.sum(picked, axis=1, keepdims=True)
        keep = pl.ds(pl.multiple_of(depth * few, few), few)
        send = pl.ds(pl.multiple_of((1 - depth) * few, few), few)
        for part in range(2):
            keep_out[part] = total[part, keep, :]
            send_out[part] = total[part, send, :].astype(BF16)

    return body


def call(body, out_shape, scratch, flops, where, *args):
    spec = pl.BlockSpec(memory_space=pltpu.VMEM)
    return pl.pallas_call(
        body,
        out_shape=out_shape,
        in_specs=[pl.BlockSpec(memory_space=pltpu.SMEM)] + [spec] * len(args),
        out_specs=[spec] * len(out_shape),
        scratch_shapes=scratch,
        compiler_params=pltpu.CompilerParams(vmem_limit_bytes=40 << 20),
        cost_estimate=pl.CostEstimate(flops=flops, bytes_accessed=8 << 20, transcendentals=0),
    )(where, *args)


def per_device(boundary, column_source, energy_weights):
    raw = boundary[0]
    _, rows, _, _, nodes = raw.shape
    half = nodes // 2
    few = rows // 2
    cluster = lax.axis_index("cluster")
    tile = lax.axis_index("tile")
    side = cluster % 2
    pair = cluster // 2 % 2
    depth = tile // 2
    core = tile % 2
    where = jnp.stack([side, depth, core, pair]).astype(jnp.int32)

    def energy_of(x, index, axis):
        return lax.dynamic_index_in_dim(x, index, axis, keepdims=False)

    one_hot = (jnp.arange(nodes, dtype=jnp.int32)[:, None] == column_source[0][None, :]).astype(BF16)

    def ordered(x):
        return jnp.einsum("irk,km->rim", x, one_hot, preferred_element_type=F32).astype(BF16)

    far_raw = exchange(energy_of(raw[0], 1 - depth, 1), "tile", 2)
    outer_all = jnp.einsum("ierk,km->erim", raw[1], one_hot, preferred_element_type=F32).astype(BF16)
    outer_all = jnp.where(depth == 0, outer_all, outer_all[::-1])
    outer_keep = lax.dynamic_slice_in_dim(outer_all, side * few, few, 2)
    outer_send = lax.dynamic_slice_in_dim(outer_all, (1 - side) * few, few, 2)
    outer_got = exchange(outer_send, "cluster", 1)
    near_own = ordered(energy_of(raw[0], depth, 1))
    near_other = exchange(near_own, "cluster", 1)
    near_own_core = exchange(near_own, "tile", 1)
    near_other_core = exchange(near_other, "tile", 1)
    outer_far = exchange(jnp.stack([outer_keep[1], outer_got[1]]), "tile", 2)
    far_own = ordered(far_raw)
    far_other = exchange(far_own, "cluster", 1)
    far_own_core = exchange(far_own, "tile", 1)
    far_other_core = exchange(far_other, "tile", 1)

    sep_rows, rest = call(
        first_level(half),
        [
            jax.ShapeDtypeStruct((2, 2 * few, nodes), BF16),
            jax.ShapeDtypeStruct((2, 2 * few, nodes), F32),
        ],
        [
            pltpu.VMEM((2, half, half), BF16),
            pltpu.VMEM((2, half, half), BF16),
            pltpu.VMEM((2, half, nodes), BF16),
            pltpu.VMEM((2, 4 * few, half), BF16),
            pltpu.VMEM((2, 4 * few, half), BF16),
        ],
        int(2.7e9),
        where,
        near_own,
        near_other,
        far_own,
        far_other,
        near_own_core,
        near_other_core,
        far_own_core,
        far_other_core,
        outer_keep[0],
        outer_got[0],
        outer_far[0],
        outer_far[1],
    )

    from_side = exchange(sep_rows, "cluster", 1)
    from_both = exchange(sep_rows, "cluster", 3)
    from_pair = exchange(sep_rows, "cluster", 2)
    mine = [sep_rows, from_side, from_pair, from_both]
    others = [exchange(x, "tile", 1) for x in mine]
    at = jnp.arange(2 * few, dtype=jnp.int32)
    row_at = pair * half + (at // few * 2 + core) * rows + side * few + at % few
    kept, sent, diagonal = call(
        last_level(half),
        [
            jax.ShapeDtypeStruct((2, few, nodes), F32),
            jax.ShapeDtypeStruct((2, few, nodes), BF16),
            jax.ShapeDtypeStruct((2 * few, 1), F32),
        ],
        [
            pltpu.VMEM((2, half, half), BF16),
            pltpu.VMEM((2, half, half), BF16),
            pltpu.VMEM((2, half, nodes), BF16),
            pltpu.VMEM((2, 2 * few, nodes), F32),
        ],
        int(1.4e9),
        where,
        *mine,
        *others,
        rest,
        row_at[:, None],
    )
    got = exchange(sent, "tile", 2)
    weighted = (diagonal[:, 0] * energy_of(energy_weights, depth, 0)).reshape(2, few)
    far_part = exchange(energy_of(weighted, 1 - depth, 0), "tile", 2)
    density = lax.psum(energy_of(weighted, depth, 0) + far_part, "energy")
    got = got.astype(F32)
    low = jnp.where(depth == 0, kept, got)
    high = jnp.where(depth == 0, got, kept)
    final_rows = jnp.stack([low, high]).transpose(2, 0, 1, 3)
    return final_rows[None], density[None]


def solution(mesh):
    placed = (P("cluster", None, "tile", "energy", None, None), P("cluster", None), P("energy"))
    return jax.shard_map(
        per_device,
        mesh=mesh,
        in_specs=placed,
        out_specs=(P("cluster", "tile", "energy", None, None), P("cluster", "tile")),
        check_vma=False,
    )
```

```python
import jax
import jax.numpy as jnp
from jax import lax
from jax.experimental import pallas as pl
from jax.experimental.pallas import tpu as pltpu
from jax.sharding import PartitionSpec as P


F32 = jnp.float32
BF16 = jnp.bfloat16
LANES = 128


def exchange(x, axis, distance):
    return lax.ppermute(x, axis, [(i, i ^ distance) for i in range(lax.axis_size(axis))])


def dot(x, y):
    return jnp.dot(x, y, preferred_element_type=F32)


def stacked(x):
    return x.reshape(2 * x.shape[1], x.shape[2])


def product(x, y_real, y_imag):
    rows = x.shape[0] // 2
    by_real, by_imag = dot(x, y_real), dot(x, y_imag)
    return by_real[:rows] - by_imag[rows:], by_imag[:rows] + by_real[rows:]


def halved(pair):
    return jnp.concatenate([pair[0].astype(BF16), pair[1].astype(BF16)], axis=0)


def at(start, size):
    return pl.ds(pl.multiple_of(start, size), size)


class Copies:
    def __init__(self, sems):
        self.sems = sems
        self.made = []

    def start(self, source, target):
        copy = pltpu.make_async_copy(source, target, self.sems.at[len(self.made)])
        copy.start()
        self.made.append(copy)
        return copy


def wait(copies):
    for copy in copies:
        copy.wait()


def call(body, out_shape, scratch, copies, flops, *args, in_vmem=(), in_smem=(), grant=40):
    spaces = [pltpu.HBM] * len(args)
    for i in in_vmem:
        spaces[i] = pltpu.VMEM
    for i in in_smem:
        spaces[i] = pltpu.SMEM
    return pl.pallas_call(
        body,
        out_shape=out_shape,
        in_specs=[pl.BlockSpec(memory_space=space) for space in spaces],
        out_specs=[pl.BlockSpec(memory_space=pltpu.VMEM)] * len(out_shape),
        scratch_shapes=scratch + [pltpu.SemaphoreType.DMA((copies,))],
        compiler_params=pltpu.CompilerParams(vmem_limit_bytes=grant << 20),
        cost_estimate=pl.CostEstimate(flops=flops, bytes_accessed=4 << 20, transcendentals=0),
    )(*args)


def places():
    cluster = lax.axis_index("cluster")
    tile = lax.axis_index("tile")
    return cluster % 2, tile // 2, tile % 2, cluster // 2 % 2


def fill_selector(column_ref, selector):
    size = selector.shape[0]
    source = lax.broadcasted_iota(jnp.int32, (size, size), 0)
    selector[...] = jnp.where(source == column_ref[...], 1.0, 0.0).astype(BF16)


def reorder(stage, selector, parted):
    count, _, nodes = stage.shape
    flat = stage[...].reshape(2 * count, nodes)
    wide = 2 * LANES
    for first in range(0, nodes, wide):
        ordered = dot(flat, selector[:, first : first + wide])
        for turn in range(2):
            parted[first // LANES + turn] = ordered[:, turn * LANES : (turn + 1) * LANES]


def lane_block(parted, block, part, first, count):
    return parted[block, pl.ds(2 * first + part, count, stride=2), :].astype(BF16)


def order_far(column_ref, raw, far_out, column, stage, selector, parted, sems):
    _, depth, _, _ = places()
    copies = Copies(sems)
    first = copies.start(column_ref, column)
    copy = copies.start(raw.at[0, 0, :, 1 - depth], stage)
    first.wait()
    fill_selector(column, selector)
    copy.wait()
    reorder(stage, selector, parted)
    count = stage.shape[0]
    for block in range(parted.shape[0]):
        for part in range(2):
            far_out[part, :, block * LANES : (block + 1) * LANES] = lane_block(
                parted, block, part, 0, count
            )


def order_rest(
    column_ref, raw, near_out, keep_out, keep_far_out, send_out,
    column, near_stage, outer_stage, selector, near_parted, outer_parted, sems,
):
    side, depth, _, _ = places()
    copies = Copies(sems)
    first = copies.start(column_ref, column)
    few = outer_stage.shape[0] // 4
    outer = []
    for row, (half, energy) in enumerate(((1, 0), (1, 1), (0, 0), (0, 1))):
        rows = at((side ^ half) * few, few)
        outer.append(
            copies.start(raw.at[0, 1, rows, depth ^ energy], outer_stage.at[pl.ds(row * few, few)])
        )
    near = copies.start(raw.at[0, 0, :, depth], near_stage)
    first.wait()
    fill_selector(column, selector)
    wait(outer)
    reorder(outer_stage, selector, outer_parted)
    blocks = outer_parted.shape[0]
    for block in range(blocks):
        lanes = slice(block * LANES, (block + 1) * LANES)
        for part in range(2):
            for energy in range(2):
                send_out[energy, part, :, lanes] = lane_block(
                    outer_parted, block, part, energy * few, few
                )
            keep_out[part, :, lanes] = lane_block(outer_parted, block, part, 2 * few, few)
            keep_far_out[part, :, lanes] = lane_block(outer_parted, block, part, 3 * few, few)
    near.wait()
    reorder(near_stage, selector, near_parted)
    for block in range(blocks):
        for part in range(2):
            near_out[part, :, block * LANES : (block + 1) * LANES] = lane_block(
                near_parted, block, part, 0, near_stage.shape[0]
            )


def assemble(parts, interior):
    for part in range(2):
        interior[part] = (parts[0, part].astype(F32) + parts[1, part].astype(F32)).astype(BF16)


def guess(interior, approx):
    size = interior.shape[1]
    real = interior[0].astype(F32)
    imag = interior[1].astype(F32)

    def on_diagonal(count):
        return lax.broadcasted_iota(jnp.int32, (count, count), 0) == lax.broadcasted_iota(
            jnp.int32, (count, count), 1
        )

    block_diag = on_diagonal(LANES)

    def diagonal(values, axis):
        found = []
        for first in range(0, size, LANES):
            span = slice(first, first + LANES)
            block = jnp.where(block_diag, values[span, span], 0.0)
            found.append(jnp.sum(block, axis=axis, keepdims=True))
        return jnp.concatenate(found, axis=1 - axis)

    def reciprocal(axis):
        diag_real = diagonal(real, axis)
        diag_imag = diagonal(imag, axis)
        denom = diag_real * diag_real + diag_imag * diag_imag
        return diag_real / denom, -diag_imag / denom

    col_real, col_imag = reciprocal(0)
    row_real, row_imag = reciprocal(1)
    temp_real = real * col_real - imag * col_imag
    temp_imag = real * col_imag + imag * col_real
    prod_real = row_real * temp_real - row_imag * temp_imag
    prod_imag = row_real * temp_imag + row_imag * temp_real
    on_diag = on_diagonal(size)
    approx[0] = (jnp.where(on_diag, 2.0 * row_real, 0.0) - prod_real).astype(BF16)
    approx[1] = (jnp.where(on_diag, 2.0 * row_imag, 0.0) - prod_imag).astype(BF16)


def eliminate(left, interior, approx):
    applied = product(left, approx[0], approx[1])
    middle = halved(product(halved(applied), interior[0], interior[1]))
    second = product(middle, approx[0], approx[1])
    return halved((2.0 * applied[0] - second[0], 2.0 * applied[1] - second[1]))


def first_level(*refs):
    near, far = refs[0:4], refs[4:8]
    keep, got, deep = refs[8:11]
    sep_out, left_out, corner_out = refs[11:14]
    parts, interior, approx, right, left, start, sems = refs[14:]
    side, depth, core, _ = places()
    copies = Copies(sems)
    width = interior.shape[1]
    rows = near[0].shape[1]
    few = rows // 2
    lows, highs = pl.ds(0, width), pl.ds(width, width)

    def sep(columns, target):
        made = []
        for turn in range(2):
            for core_step in range(2):
                who = core_step * 2 + turn
                for step, pieces in enumerate((near, far)):
                    row = at(((depth ^ step) * 2 + (core ^ core_step)) * rows, rows)
                    made.append(
                        copies.start(pieces[who].at[:, :, columns], target.at[side ^ turn, :, row])
                    )
        return made

    def outer(columns, target):
        near_rows, far_rows = at(depth * few, few), at((1 - depth) * few, few)
        return [
            copies.start(keep.at[:, :, columns], target.at[side, :, near_rows]),
            copies.start(got.at[0, :, :, columns], target.at[1 - side, :, near_rows]),
            copies.start(deep.at[0, :, :, columns], target.at[side, :, far_rows]),
            copies.start(deep.at[1, :, :, columns], target.at[1 - side, :, far_rows]),
        ]

    from_inner = sep(lows, parts)
    from_left = outer(lows, left)
    from_cross = sep(highs, right)
    from_start = outer(highs, start)
    wait(from_inner)
    assemble(parts, interior)
    guess(interior, approx)
    wait(from_left)
    both = jnp.concatenate([left[0, 0], left[1, 0], left[0, 1], left[1, 1]], axis=0)
    reduced = eliminate(both, interior, approx)
    wait(from_cross)
    wait(from_start)
    low_taken = product(reduced, right[0, 0], right[0, 1])
    high_taken = product(reduced, right[1, 0], right[1, 1])
    for part in range(2):
        sep_out[part, :, :width] = (
            start[0, part].astype(F32) - low_taken[part][:rows]
        ).astype(BF16)
        sep_out[part, :, width:] = (-high_taken[part][:rows]).astype(BF16)
        left_out[part] = (-low_taken[part][rows:]).astype(BF16)
        corner_out[part] = start[1, part].astype(F32) - high_taken[part][rows:]


def last_level(*refs):
    pieces = refs[:8]
    left, corner, weights = refs[8:11]
    keep_out, send_out, keep_diag_out, send_diag_out = refs[11:15]
    parts, interior, approx, right, total, diag, sems = refs[15:]
    side, depth, core, pair = places()
    copies = Copies(sems)
    width = interior.shape[1]
    rows = corner.shape[1]
    few = rows // 2

    def spread(columns, target):
        made = []
        for who, piece in enumerate(pieces):
            core_step, pair_step, side_step = who // 4, who // 2 % 2, who % 2
            for deep in range(2):
                row = (deep * 2 + (core ^ core_step)) * rows + (side ^ side_step) * few
                made.append(
                    copies.start(
                        piece.at[:, pl.ds(deep * few, few), columns],
                        target.at[pair ^ pair_step, :, at(row, few)],
                    )
                )
        return made

    from_inner = spread(pl.ds(0, width), parts)
    from_cross = spread(pl.ds(width, width), right)
    wait(from_inner)
    assemble(parts, interior)
    guess(interior, approx)
    reduced = eliminate(stacked(left[...]), interior, approx)
    wait(from_cross)
    for owner in range(2):
        taken = product(reduced, right[owner, 0], right[owner, 1])
        for part in range(2):
            start = jnp.where(pair == owner, corner[part], 0.0)
            total[part, :, owner * width : (owner + 1) * width] = start - taken[part]
    own = total[1, :, at(pair * width, width)]
    row_of = lax.broadcasted_iota(jnp.int32, (few, LANES), 0) + side * few
    lane_of = lax.broadcasted_iota(jnp.int32, (few, LANES), 1)
    for deep in range(2):
        for_core = [
            own[deep * few : (deep + 1) * few, tile * LANES : (tile + 1) * LANES]
            for tile in (deep * 2, deep * 2 + 1)
        ]
        block = jnp.where(core == 0, for_core[0], for_core[1])
        found = jnp.sum(jnp.where(row_of == lane_of, block, 0.0), axis=0, keepdims=True)
        diag[deep] = found * weights[depth]
    keep_diag_out[...] = diag[depth]
    send_diag_out[...] = diag[1 - depth]
    near_rows, far_rows = at(depth * few, few), at((1 - depth) * few, few)
    for part in range(2):
        send_out[part] = total[part, far_rows, :].astype(BF16)
        keep_out[part] = total[part, near_rows, :]


def after(x, *others):
    return lax.optimization_barrier((x,) + others)[0]


def compute(boundary, column_source, energy_weights):
    _, _, rows, _, _, nodes = boundary.shape
    half = nodes // 2
    few = rows // 2
    depth = lax.axis_index("tile") // 2

    def bf16(*shape):
        return jax.ShapeDtypeStruct(shape, BF16)

    def f32(*shape):
        return jax.ShapeDtypeStruct(shape, F32)

    selector = pltpu.VMEM((nodes, nodes), BF16)
    column = pltpu.VMEM((1, nodes), jnp.int32)
    lane_blocks = nodes // LANES
    (far_raw,) = call(
        order_far,
        [bf16(2, rows, nodes)],
        [
            column,
            pltpu.VMEM((rows, 2, nodes), BF16),
            selector,
            pltpu.VMEM((lane_blocks, 2 * rows, LANES), F32),
        ],
        2,
        int(1e9),
        column_source,
        boundary,
        grant=63,
    )
    far = exchange(far_raw, "tile", 2)
    near, keep, keep_far, send = call(
        order_rest,
        [bf16(2, rows, nodes), bf16(2, few, nodes), bf16(2, few, nodes), bf16(2, 2, few, nodes)],
        [
            column,
            pltpu.VMEM((rows, 2, nodes), BF16),
            pltpu.VMEM((4 * few, 2, nodes), BF16),
            selector,
            pltpu.VMEM((lane_blocks, 2 * rows, LANES), F32),
            pltpu.VMEM((lane_blocks, 8 * few, LANES), F32),
        ],
        6,
        int(2e9),
        after(column_source, far_raw),
        boundary,
        grant=56,
    )
    got = exchange(send, "cluster", 1)
    near_core = exchange(near, "tile", 1)
    near_side = exchange(after(near, got), "cluster", 1)
    to_deep = jnp.stack([keep_far, got[1]])
    deep = exchange(to_deep, "tile", 2)
    near_side_core = exchange(near_side, "tile", 1)
    far = after(far, to_deep)
    far_side = exchange(far, "cluster", 1)
    far_core = exchange(far, "tile", 1)
    far_side_core = exchange(far_side, "tile", 1)

    weights = jnp.concatenate([energy_weights, energy_weights])

    weights = jnp.concatenate([energy_weights, energy_weights])

    weights = jnp.concatenate([energy_weights, energy_weights])

    square = pltpu.VMEM((2, half, half), BF16)
    squares = pltpu.VMEM((2, 2, half, half), BF16)
    sep_rows, left, corner = call(
        first_level,
        [bf16(2, rows, nodes), bf16(2, rows, half), f32(2, rows, half)],
        [
            squares,
            square,
            square,
            squares,
            pltpu.VMEM((2, 2, rows, half), BF16),
            pltpu.VMEM((2, 2, rows, half), BF16),
        ],
        24,
        int(2.7e9),
        near,
        near_side,
        near_core,
        near_side_core,
        far,
        far_side,
        far_core,
        far_side_core,
        keep,
        got,
        deep,
    )
    mine = [sep_rows] + [exchange(sep_rows, "cluster", distance) for distance in (1, 2, 3)]
    kept, sent, kept_diag, sent_diag = call(
        last_level,
        [f32(2, few, nodes), bf16(2, few, nodes), f32(1, LANES), f32(1, LANES)],
        [
            squares,
            square,
            square,
            squares,
            pltpu.VMEM((2, rows, nodes), F32),
            pltpu.VMEM((2, 1, LANES), F32),
        ],
        32,
        int(1.4e9),
        *mine,
        *[exchange(x, "tile", 1) for x in mine],
        left,
        corner,
        weights,
        in_vmem=(8, 9),
        in_smem=(10,),
    )
    got_diag = exchange(sent_diag, "tile", 2)
    got_rows = exchange(sent, "tile", 2).astype(F32)
    density = lax.psum(kept_diag + got_diag, "energy")
    density = density[:, :few] + density[:, few:]
    low = jnp.where(depth == 0, kept, got_rows)
    high = jnp.where(depth == 0, got_rows, kept)
    final_rows = jnp.stack([low, high]).transpose(2, 0, 1, 3)
    return final_rows[None], density


def solution(mesh):
    placed = (P("cluster", None, "tile", "energy", None, None), P("cluster", None), P("energy"))
    return jax.shard_map(
        compute,
        mesh=mesh,
        in_specs=placed,
        out_specs=(P("cluster", "tile", "energy", None, None), P("cluster", "tile")),
        check_vma=False,
    )
```

```python
import jax
import jax.numpy as jnp
from jax import lax
from jax.experimental import pallas as pl
from jax.experimental.pallas import tpu as pltpu
from jax.sharding import PartitionSpec as P


F32 = jnp.float32
BF16 = jnp.bfloat16
LANES = 128


def exchange(x, axis, distance):
    return lax.ppermute(x, axis, [(i, i ^ distance) for i in range(lax.axis_size(axis))])


def dot(x, y):
    return jnp.dot(x, y, preferred_element_type=F32)


def stacked(x):
    return x.reshape(2 * x.shape[1], x.shape[2])


def product(x, y_real, y_imag):
    rows = x.shape[0] // 2
    by_real, by_imag = dot(x, y_real), dot(x, y_imag)
    return by_real[:rows] - by_imag[rows:], by_imag[:rows] + by_real[rows:]


def halved(pair):
    return jnp.concatenate([pair[0].astype(BF16), pair[1].astype(BF16)], axis=0)


def at(start, size):
    return pl.ds(pl.multiple_of(start, size), size)


class Copies:
    def __init__(self, sems):
        self.sems = sems
        self.made = []

    def start(self, source, target):
        copy = pltpu.make_async_copy(source, target, self.sems.at[len(self.made)])
        copy.start()
        self.made.append(copy)
        return copy


def wait(copies):
    for copy in copies:
        copy.wait()


def call(body, out_shape, scratch, copies, flops, *args, in_vmem=(), in_smem=(), grant=40):
    spaces = [pltpu.HBM] * len(args)
    for i in in_vmem:
        spaces[i] = pltpu.VMEM
    for i in in_smem:
        spaces[i] = pltpu.SMEM
    return pl.pallas_call(
        body,
        out_shape=out_shape,
        in_specs=[pl.BlockSpec(memory_space=space) for space in spaces],
        out_specs=[pl.BlockSpec(memory_space=pltpu.VMEM)] * len(out_shape),
        scratch_shapes=scratch + [pltpu.SemaphoreType.DMA((copies,))],
        compiler_params=pltpu.CompilerParams(vmem_limit_bytes=grant << 20),
        cost_estimate=pl.CostEstimate(flops=flops, bytes_accessed=4 << 20, transcendentals=0),
    )(*args)


def places():
    cluster = lax.axis_index("cluster")
    tile = lax.axis_index("tile")
    return cluster % 2, tile // 2, tile % 2, cluster // 2 % 2


def fill_selector(column_ref, selector):
    size = selector.shape[0]
    source = lax.broadcasted_iota(jnp.int32, (size, size), 0)
    selector[...] = jnp.where(source == column_ref[...], 1.0, 0.0).astype(BF16)


def reorder(stage, selector, parted):
    count, _, nodes = stage.shape
    flat = stage[...].reshape(2 * count, nodes)
    wide = 2 * LANES
    for first in range(0, nodes, wide):
        ordered = dot(flat, selector[:, first : first + wide])
        for turn in range(2):
            parted[first // LANES + turn] = ordered[:, turn * LANES : (turn + 1) * LANES]


def lane_block(parted, block, part, first, count):
    return parted[block, pl.ds(2 * first + part, count, stride=2), :].astype(BF16)


def order_first(
    column_ref, raw, far_out, send_out,
    column, far_stage, send_stage, selector, far_parted, send_parted, sems,
):
    side, depth, _, _ = places()
    copies = Copies(sems)
    first = copies.start(column_ref, column)
    far = copies.start(raw.at[0, 0, :, 1 - depth], far_stage)
    few = send_stage.shape[0] // 2
    rows = at((1 - side) * few, few)
    sent = [
        copies.start(raw.at[0, 1, rows, depth ^ turn], send_stage.at[pl.ds(turn * few, few)])
        for turn in range(2)
    ]
    first.wait()
    fill_selector(column, selector)
    far.wait()
    reorder(far_stage, selector, far_parted)
    blocks = far_parted.shape[0]
    for block in range(blocks):
        lanes = slice(block * LANES, (block + 1) * LANES)
        for part in range(2):
            far_out[part, :, lanes] = lane_block(far_parted, block, part, 0, far_stage.shape[0])
    wait(sent)
    reorder(send_stage, selector, send_parted)
    for block in range(blocks):
        lanes = slice(block * LANES, (block + 1) * LANES)
        for part in range(2):
            for turn in range(2):
                send_out[turn, part, :, lanes] = lane_block(
                    send_parted, block, part, turn * few, few
                )


def order_near(
    column_ref, raw, near_out, keep_out, keep_far_out,
    column, near_stage, keep_stage, selector, near_parted, keep_parted, sems,
):
    side, depth, _, _ = places()
    copies = Copies(sems)
    first = copies.start(column_ref, column)
    few = keep_stage.shape[0] // 2
    rows = at(side * few, few)
    kept = [
        copies.start(raw.at[0, 1, rows, depth ^ turn], keep_stage.at[pl.ds(turn * few, few)])
        for turn in range(2)
    ]
    near = copies.start(raw.at[0, 0, :, depth], near_stage)
    first.wait()
    fill_selector(column, selector)
    wait(kept)
    reorder(keep_stage, selector, keep_parted)
    near.wait()
    reorder(near_stage, selector, near_parted)
    blocks = near_parted.shape[0]
    for block in range(blocks):
        lanes = slice(block * LANES, (block + 1) * LANES)
        for part in range(2):
            keep_out[part, :, lanes] = lane_block(keep_parted, block, part, 0, few)
            keep_far_out[part, :, lanes] = lane_block(keep_parted, block, part, few, few)
            near_out[part, :, lanes] = lane_block(near_parted, block, part, 0, near_stage.shape[0])


def assemble(parts, interior):
    for part in range(2):
        interior[part] = (parts[0, part].astype(F32) + parts[1, part].astype(F32)).astype(BF16)


def guess(interior, approx):
    size = interior.shape[1]
    real = interior[0].astype(F32)
    imag = interior[1].astype(F32)

    def on_diagonal(count):
        return lax.broadcasted_iota(jnp.int32, (count, count), 0) == lax.broadcasted_iota(
            jnp.int32, (count, count), 1
        )

    block_diag = on_diagonal(LANES)

    def diagonal(values, axis):
        found = []
        for first in range(0, size, LANES):
            span = slice(first, first + LANES)
            block = jnp.where(block_diag, values[span, span], 0.0)
            found.append(jnp.sum(block, axis=axis, keepdims=True))
        return jnp.concatenate(found, axis=1 - axis)

    def reciprocal(axis):
        diag_real = diagonal(real, axis)
        diag_imag = diagonal(imag, axis)
        denom = diag_real * diag_real + diag_imag * diag_imag
        return diag_real / denom, -diag_imag / denom

    col_real, col_imag = reciprocal(0)
    row_real, row_imag = reciprocal(1)
    temp_real = real * col_real - imag * col_imag
    temp_imag = real * col_imag + imag * col_real
    prod_real = row_real * temp_real - row_imag * temp_imag
    prod_imag = row_real * temp_imag + row_imag * temp_real
    on_diag = on_diagonal(size)
    approx[0] = (jnp.where(on_diag, 2.0 * row_real, 0.0) - prod_real).astype(BF16)
    approx[1] = (jnp.where(on_diag, 2.0 * row_imag, 0.0) - prod_imag).astype(BF16)


def eliminate(left, interior, approx):
    applied = product(left, approx[0], approx[1])
    middle = halved(product(halved(applied), interior[0], interior[1]))
    second = product(middle, approx[0], approx[1])
    return halved((2.0 * applied[0] - second[0], 2.0 * applied[1] - second[1]))


def merged(left, start, interior, approx, right, sep_out, left_out, corner_out):
    width = interior.shape[1]
    few = sep_out.shape[1]
    both = jnp.concatenate([left[0, 0], left[1, 0], left[0, 1], left[1, 1]], axis=0)
    reduced = eliminate(both, interior, approx)
    low_taken = product(reduced, right[0, 0], right[0, 1])
    high_taken = product(reduced, right[1, 0], right[1, 1])
    for part in range(2):
        sep_out[part, :, :width] = (start[0, part].astype(F32) - low_taken[part][:few]).astype(BF16)
        sep_out[part, :, width:] = (-high_taken[part][:few]).astype(BF16)
        left_out[part] = (-low_taken[part][few:]).astype(BF16)
        corner_out[part] = start[1, part].astype(F32) - high_taken[part][few:]


def near_level(*refs):
    near, far = refs[0:4], refs[4:8]
    keep, got = refs[8:10]
    sep_out, left_out, corner_out, interior, approx, right = refs[10:16]
    parts, left, start, sems = refs[16:]
    side, depth, core, _ = places()
    copies = Copies(sems)
    width = interior.shape[1]
    rows = near[0].shape[1]
    lows, highs = pl.ds(0, width), pl.ds(width, width)

    def sep(columns, target):
        made = []
        for turn in range(2):
            for core_step in range(2):
                who = core_step * 2 + turn
                for step, pieces in enumerate((near, far)):
                    row = at(((depth ^ step) * 2 + (core ^ core_step)) * rows, rows)
                    made.append(
                        copies.start(pieces[who].at[:, :, columns], target.at[side ^ turn, :, row])
                    )
        return made

    def outer(columns, target):
        return [
            copies.start(keep.at[:, :, columns], target.at[side]),
            copies.start(got.at[0, :, :, columns], target.at[1 - side]),
        ]

    from_inner = sep(lows, parts)
    from_outer = outer(lows, left)
    from_cross = sep(highs, right)
    from_outer += outer(highs, start)
    wait(from_inner)
    assemble(parts, interior)
    guess(interior, approx)
    wait(from_outer)
    wait(from_cross)
    merged(left, start, interior, approx, right, sep_out, left_out, corner_out)


def far_level(*refs):
    deep, interior, approx, right, left_near, corner_near = refs[:6]
    sep_out, left_both, corner_both = refs[6:9]
    left, start, sems = refs[9:]
    few = deep.shape[2]
    left_both[:, :few] = left_near[...]
    corner_both[:, :few] = corner_near[...]
    left_out, corner_out = left_both.at[:, few:], corner_both.at[:, few:]
    side, _, _, _ = places()
    copies = Copies(sems)
    width = interior.shape[1]
    made = []
    for turn in range(2):
        for first, target in ((0, left), (width, start)):
            made.append(
                copies.start(deep.at[turn, :, :, pl.ds(first, width)], target.at[side ^ turn])
            )
    wait(made)
    merged(left, start, interior, approx, right, sep_out, left_out, corner_out)


def last_level(*refs):
    pieces = refs[:16]
    left, corner, weights = refs[16:19]
    keep_out, send_out, keep_diag_out, send_diag_out = refs[19:23]
    parts, interior, approx, right, total, sems = refs[23:]
    side, depth, core, pair = places()
    copies = Copies(sems)
    width = interior.shape[1]
    rows = corner.shape[1]
    few = rows // 2

    def spread(columns, target):
        made = []
        for who, piece in enumerate(pieces):
            core_step, step, pair_step, side_step = who // 8, who // 4 % 2, who // 2 % 2, who % 2
            row = ((depth ^ step) * 2 + (core ^ core_step)) * rows + (side ^ side_step) * few
            made.append(
                copies.start(
                    piece.at[:, :, columns], target.at[pair ^ pair_step, :, at(row, few)]
                )
            )
        return made

    from_inner = spread(pl.ds(0, width), parts)
    from_cross = spread(pl.ds(width, width), right)
    wait(from_inner)
    assemble(parts, interior)
    guess(interior, approx)
    reduced = eliminate(stacked(left[...]), interior, approx)
    wait(from_cross)
    for owner in range(2):
        taken = product(reduced, right[owner, 0], right[owner, 1])
        for part in range(2):
            start = jnp.where(pair == owner, corner[part], 0.0)
            total[part, :, owner * width : (owner + 1) * width] = start - taken[part]
    row_of = lax.broadcasted_iota(jnp.int32, (few, LANES), 0) + side * few
    lane_of = lax.broadcasted_iota(jnp.int32, (few, LANES), 1)
    for step, out in enumerate((keep_diag_out, send_diag_out)):
        column = pair * width + ((depth ^ step) * 2 + core) * LANES
        block = total[1, step * few : (step + 1) * few, at(column, LANES)]
        found = jnp.sum(jnp.where(row_of == lane_of, block, 0.0), axis=0, keepdims=True)
        out[...] = found * weights[depth]
    for part in range(2):
        send_out[part] = total[part, few:, :].astype(BF16)
        keep_out[part] = total[part, :few, :]


def after(x, *others):
    return lax.optimization_barrier((x,) + others)[0]


def compute(boundary, column_source, energy_weights):
    _, _, rows, _, _, nodes = boundary.shape
    half = nodes // 2
    few = rows // 2
    depth = lax.axis_index("tile") // 2

    def bf16(*shape):
        return jax.ShapeDtypeStruct(shape, BF16)

    def f32(*shape):
        return jax.ShapeDtypeStruct(shape, F32)

    selector = pltpu.VMEM((nodes, nodes), BF16)
    column = pltpu.VMEM((1, nodes), jnp.int32)
    stage = pltpu.VMEM((rows, 2, nodes), BF16)
    parted = pltpu.VMEM((nodes // LANES, 2 * rows, LANES), F32)
    far_raw, send = call(
        order_first,
        [bf16(2, rows, nodes), bf16(2, 2, few, nodes)],
        [column, stage, stage, selector, parted, parted],
        4,
        int(2e9),
        column_source,
        boundary,
        grant=62,
    )
    far = exchange(far_raw, "tile", 2)
    got = exchange(send, "cluster", 1)
    near, keep, keep_far = call(
        order_near,
        [bf16(2, rows, nodes), bf16(2, few, nodes), bf16(2, few, nodes)],
        [column, stage, stage, selector, parted, parted],
        4,
        int(2e9),
        after(column_source, far_raw),
        boundary,
        grant=40,
    )
    near_core = exchange(near, "tile", 1)
    near_side = exchange(after(near, got), "cluster", 1)
    to_deep = jnp.stack([keep_far, after(got[1], near_side)])
    deep = exchange(to_deep, "tile", 2)
    near_side_core = exchange(near_side, "tile", 1)
    far = after(far, to_deep)
    far_side = exchange(far, "cluster", 1)
    far_core = exchange(far, "tile", 1)
    far_side_core = exchange(far_side, "tile", 1)
    weights = jnp.concatenate([energy_weights, energy_weights])

    square = pltpu.VMEM((2, half, half), BF16)
    squares = pltpu.VMEM((2, 2, half, half), BF16)
    rim = pltpu.VMEM((2, 2, few, half), BF16)
    results = [bf16(2, few, nodes), bf16(2, few, half), f32(2, few, half)]
    sep_near, left_near, corner_near, interior, approx, right = call(
        near_level,
        results + [bf16(2, half, half), bf16(2, half, half), bf16(2, 2, half, half)],
        [squares, rim, rim],
        20,
        int(2e9),
        near,
        near_side,
        near_core,
        near_side_core,
        far,
        far_side,
        far_core,
        far_side_core,
        keep,
        got,
    )
    sep_far, left, corner = call(
        far_level,
        [bf16(2, few, nodes), bf16(2, rows, half), f32(2, rows, half)],
        [rim, rim],
        4,
        int(1.4e9),
        deep,
        interior,
        approx,
        right,
        left_near,
        corner_near,
        in_vmem=(1, 2, 3, 4, 5),
    )

    def around(x):
        return [x] + [exchange(x, "cluster", distance) for distance in (1, 2, 3)]

    near_mine = around(sep_near)
    far_mine = around(sep_far)
    near_others = [exchange(x, "tile", 1) for x in near_mine]
    far_others = [exchange(x, "tile", 1) for x in far_mine]
    kept, sent, kept_diag, sent_diag = call(
        last_level,
        [f32(2, few, nodes), bf16(2, few, nodes), f32(1, LANES), f32(1, LANES)],
        [
            squares,
            square,
            square,
            squares,
            pltpu.VMEM((2, rows, nodes), F32),
        ],
        32,
        int(1.4e9),
        *near_mine,
        *far_mine,
        *near_others,
        *far_others,
        left,
        corner,
        weights,
        in_vmem=(16, 17),
        in_smem=(18,),
        grant=40,
    )
    mine_diag = kept_diag + exchange(sent_diag, "tile", 2)
    got_rows = exchange(sent, "tile", 2).astype(F32)
    density = mine_diag
    for distance in (1, 2):
        density = density + exchange(density, "energy", distance)
    density = density[:, :few] + density[:, few:]
    low = jnp.where(depth == 0, kept, got_rows)
    high = jnp.where(depth == 0, got_rows, kept)
    final_rows = jnp.stack([low, high]).transpose(2, 0, 1, 3)
    return final_rows[None], density


def solution(mesh):
    placed = (P("cluster", None, "tile", "energy", None, None), P("cluster", None), P("energy"))
    return jax.shard_map(
        compute,
        mesh=mesh,
        in_specs=placed,
        out_specs=(P("cluster", "tile", "energy", None, None), P("cluster", "tile")),
        check_vma=False,
    )
```

```python
import jax
import jax.numpy as jnp
from jax import lax
from jax.experimental import pallas as pl
from jax.experimental.pallas import tpu as pltpu
from jax.sharding import PartitionSpec as P


F32 = jnp.float32
BF16 = jnp.bfloat16
LANES = 128


def exchange(x, axis, distance):
    return lax.ppermute(x, axis, [(i, i ^ distance) for i in range(lax.axis_size(axis))])


def dot(x, y):
    return jnp.dot(x, y, preferred_element_type=F32)


def stacked(x):
    return x.reshape(2 * x.shape[1], x.shape[2])


def product(x, y_real, y_imag):
    rows = x.shape[0] // 2
    by_real, by_imag = dot(x, y_real), dot(x, y_imag)
    return by_real[:rows] - by_imag[rows:], by_imag[:rows] + by_real[rows:]


def halved(pair):
    return jnp.concatenate([pair[0].astype(BF16), pair[1].astype(BF16)], axis=0)


def at(start, size):
    return pl.ds(pl.multiple_of(start, size), size)


class Copies:
    def __init__(self, sems):
        self.sems = sems
        self.made = []

    def start(self, source, target):
        copy = pltpu.make_async_copy(source, target, self.sems.at[len(self.made)])
        copy.start()
        self.made.append(copy)
        return copy


def wait(copies):
    for copy in copies:
        copy.wait()


def call(body, out_shape, scratch, copies, flops, *args, in_vmem=(), in_smem=(), grant=40):
    spaces = [pltpu.HBM] * len(args)
    for i in in_vmem:
        spaces[i] = pltpu.VMEM
    for i in in_smem:
        spaces[i] = pltpu.SMEM
    return pl.pallas_call(
        body,
        out_shape=out_shape,
        in_specs=[pl.BlockSpec(memory_space=space) for space in spaces],
        out_specs=[pl.BlockSpec(memory_space=pltpu.VMEM)] * len(out_shape),
        scratch_shapes=scratch + [pltpu.SemaphoreType.DMA((copies,))],
        compiler_params=pltpu.CompilerParams(vmem_limit_bytes=grant << 20),
        cost_estimate=pl.CostEstimate(flops=flops, bytes_accessed=4 << 20, transcendentals=0),
    )(*args)


def places():
    cluster = lax.axis_index("cluster")
    tile = lax.axis_index("tile")
    return cluster % 2, tile // 2, tile % 2, cluster // 2 % 2


def fill_selector(column_ref, selector):
    size = selector.shape[0]
    source = lax.broadcasted_iota(jnp.int32, (size, size), 0)
    selector[...] = jnp.where(source == column_ref[...], 1.0, 0.0).astype(BF16)


def reorder(stage, selector, parted):
    count, _, nodes = stage.shape
    flat = stage[...].reshape(2 * count, nodes)
    wide = 2 * LANES
    for first in range(0, nodes, wide):
        ordered = dot(flat, selector[:, first : first + wide])
        for turn in range(2):
            parted[first // LANES + turn] = ordered[:, turn * LANES : (turn + 1) * LANES]


def lane_block(parted, block, part, first, count):
    return parted[block, pl.ds(2 * first + part, count, stride=2), :].astype(BF16)


def order_first(
    column_ref, raw, send_out, inner_out, cross_out,
    column, send_stage, own_stage, selector, send_parted, own_parted, sems,
):
    side, _, _, _ = places()
    copies = Copies(sems)
    first = copies.start(column_ref, column)
    sent = copies.start(raw.at[0, 0, :, 1 - side], send_stage)
    owned = copies.start(raw.at[0, 0, :, side], own_stage)
    first.wait()
    fill_selector(column, selector)
    sent.wait()
    reorder(send_stage, selector, send_parted)
    owned.wait()
    reorder(own_stage, selector, own_parted)
    blocks = send_parted.shape[0]
    count = send_stage.shape[0]
    for block in range(blocks):
        lanes = slice(block * LANES, (block + 1) * LANES)
        out = (inner_out, cross_out)[2 * block // blocks]
        column_at = block % (blocks // 2) * LANES
        for part in range(2):
            send_out[part, :, lanes] = lane_block(send_parted, block, part, 0, count)
            out[part, :, column_at : column_at + LANES] = lane_block(
                own_parted, block, part, 0, count
            )


def order_second(
    column_ref, raw, send_out, keep_out,
    column, send_stage, own_stage, selector, send_parted, own_parted, sems,
):
    side, _, _, _ = places()
    copies = Copies(sems)
    first = copies.start(column_ref, column)
    sent = copies.start(raw.at[0, 1, :, 1 - side], send_stage)
    owned = copies.start(raw.at[0, 1, :, side], own_stage)
    first.wait()
    fill_selector(column, selector)
    sent.wait()
    reorder(send_stage, selector, send_parted)
    owned.wait()
    reorder(own_stage, selector, own_parted)
    count = send_stage.shape[0]
    for block in range(send_parted.shape[0]):
        lanes = slice(block * LANES, (block + 1) * LANES)
        for part in range(2):
            send_out[part, :, lanes] = lane_block(send_parted, block, part, 0, count)
            keep_out[part, :, lanes] = lane_block(own_parted, block, part, 0, count)


def guess(interior, approx):
    size = interior.shape[1]
    real = interior[0].astype(F32)
    imag = interior[1].astype(F32)

    def on_diagonal(count):
        return lax.broadcasted_iota(jnp.int32, (count, count), 0) == lax.broadcasted_iota(
            jnp.int32, (count, count), 1
        )

    block_diag = on_diagonal(LANES)

    def diagonal(values, axis):
        found = []
        for first in range(0, size, LANES):
            span = slice(first, first + LANES)
            block = jnp.where(block_diag, values[span, span], 0.0)
            found.append(jnp.sum(block, axis=axis, keepdims=True))
        return jnp.concatenate(found, axis=1 - axis)

    def reciprocal(axis):
        diag_real = diagonal(real, axis)
        diag_imag = diagonal(imag, axis)
        denom = diag_real * diag_real + diag_imag * diag_imag
        return diag_real / denom, -diag_imag / denom

    col_real, col_imag = reciprocal(0)
    row_real, row_imag = reciprocal(1)
    temp_real = real * col_real - imag * col_imag
    temp_imag = real * col_imag + imag * col_real
    prod_real = row_real * temp_real - row_imag * temp_imag
    prod_imag = row_real * temp_imag + row_imag * temp_real
    on_diag = on_diagonal(size)
    approx[0] = (jnp.where(on_diag, 2.0 * row_real, 0.0) - prod_real).astype(BF16)
    approx[1] = (jnp.where(on_diag, 2.0 * row_imag, 0.0) - prod_imag).astype(BF16)


def eliminate(left, interior, approx):
    applied = product(left, approx[0], approx[1])
    middle = halved(product(halved(applied), interior[0], interior[1]))
    second = product(middle, approx[0], approx[1])
    return halved((2.0 * applied[0] - second[0], 2.0 * applied[1] - second[1]))


def spread(copies, pieces, columns, target):
    _, depth, core, _ = places()
    rows = pieces[0].shape[1]
    made = []
    for who, piece in enumerate(pieces):
        row = at(((depth ^ (who % 2)) * 2 + (core ^ (who // 2))) * rows, rows)
        made.append(copies.start(piece.at[:, :, columns], target.at[:, row]))
    return made


def first_level(*refs):
    owns, mixed = refs[0:4], refs[4:8]
    keep, got = refs[8:10]
    inner_out, cross_out, left_out, corner_out = refs[10:14]
    interior, approx, right, left, start, sems = refs[14:]
    side, _, _, _ = places()
    copies = Copies(sems)
    width = interior.shape[1]
    rows = keep.shape[1]
    lows, highs = pl.ds(0, width), pl.ds(width, width)
    from_inner = spread(copies, mixed, lows, interior)
    from_outer = [
        copies.start(keep.at[:, :, lows], left.at[side]),
        copies.start(got.at[:, :, lows], left.at[1 - side]),
    ]
    from_cross = spread(copies, owns, lows, right.at[side])
    from_cross += spread(copies, mixed, highs, right.at[1 - side])
    from_cross += [
        copies.start(keep.at[:, :, highs], start.at[side]),
        copies.start(got.at[:, :, highs], start.at[1 - side]),
    ]
    wait(from_inner)
    guess(interior, approx)
    wait(from_outer)
    both = jnp.concatenate([left[0, 0], left[1, 0], left[0, 1], left[1, 1]], axis=0)
    reduced = eliminate(both, interior, approx)
    wait(from_cross)
    low_taken = product(reduced, right[0, 0], right[0, 1])
    high_taken = product(reduced, right[1, 0], right[1, 1])
    for part in range(2):
        inner_out[part] = (start[0, part].astype(F32) - low_taken[part][:rows]).astype(BF16)
        cross_out[part] = (-high_taken[part][:rows]).astype(BF16)
        left_out[part] = (-low_taken[part][rows:]).astype(BF16)
        corner_out[part] = start[1, part].astype(F32) - high_taken[part][rows:]


def last_level(*refs):
    sums, owns, others = refs[0:4], refs[4:8], refs[8:12]
    left, corner, weights = refs[12:15]
    keep_out, send_out, diag_out = refs[15:18]
    interior, approx, right, total, sems = refs[18:]
    side, depth, core, pair = places()
    copies = Copies(sems)
    width = interior.shape[1]
    rows = corner.shape[1]
    few = rows // 2
    every = pl.ds(0, width)
    from_inner = spread(copies, sums, every, interior)
    from_cross = spread(copies, owns, every, right.at[pair])
    from_cross += spread(copies, others, every, right.at[1 - pair])
    wait(from_inner)
    guess(interior, approx)
    reduced = eliminate(stacked(left[...]), interior, approx)
    wait(from_cross)
    for owner in range(2):
        taken = product(reduced, right[owner, 0], right[owner, 1])
        for part in range(2):
            start = jnp.where(pair == owner, corner[part], 0.0)
            total[part, :, owner * width : (owner + 1) * width] = start - taken[part]
    block = total[1, :, at(pair * width + (depth * 2 + core) * LANES, LANES)]
    row_of = lax.broadcasted_iota(jnp.int32, (rows, LANES), 0)
    lane_of = lax.broadcasted_iota(jnp.int32, (rows, LANES), 1)
    found = jnp.sum(jnp.where(row_of == lane_of, block, 0.0), axis=0, keepdims=True)
    diag_out[...] = found * weights[side]
    keep_rows, send_rows = at(side * few, few), at((1 - side) * few, few)
    for part in range(2):
        send_out[part] = total[part, send_rows, :].astype(BF16)
        keep_out[part] = total[part, keep_rows, :]


def after(x, *others):
    return lax.optimization_barrier((x,) + others)[0]


def compute(boundary, column_source, energy_weights):
    _, _, rows, _, _, nodes = boundary.shape
    half = nodes // 2
    few = rows // 2
    side = lax.axis_index("cluster") % 2

    def bf16(*shape):
        return jax.ShapeDtypeStruct(shape, BF16)

    def f32(*shape):
        return jax.ShapeDtypeStruct(shape, F32)

    def total_of(x, y):
        return (x.astype(F32) + y.astype(F32)).astype(BF16)

    selector = pltpu.VMEM((nodes, nodes), BF16)
    column = pltpu.VMEM((1, nodes), jnp.int32)
    stage = pltpu.VMEM((rows, 2, nodes), BF16)
    parted = pltpu.VMEM((nodes // LANES, 2 * rows, LANES), F32)
    ordering = [column, stage, stage, selector, parted, parted]
    first, own_inner, own = call(
        order_first,
        [bf16(2, rows, nodes), bf16(2, rows, half), bf16(2, rows, half)],
        ordering,
        3,
        int(2e9),
        column_source,
        boundary,
        grant=62,
    )
    got = exchange(first, "cluster", 1)
    own_far = exchange(own, "tile", 2)
    outer, keep = call(
        order_second,
        [bf16(2, rows, nodes), bf16(2, rows, nodes)],
        ordering,
        3,
        int(2e9),
        after(column_source, own),
        boundary,
    )
    outer_got = exchange(after(outer, got), "cluster", 1)
    mixed = jnp.concatenate([total_of(own_inner, got[..., :half]), got[..., half:]], axis=2)
    mixed_far = exchange(mixed, "tile", 2)
    owns = [own, own_far]
    owns += [exchange(own, "tile", 1), exchange(own_far, "tile", 1)]
    mixes = [mixed, mixed_far]
    mixes += [exchange(mixed, "tile", 1), exchange(mixed_far, "tile", 1)]

    square = pltpu.VMEM((2, half, half), BF16)
    squares = pltpu.VMEM((2, 2, half, half), BF16)
    rim = pltpu.VMEM((2, 2, rows, half), BF16)
    inner, cross, left, corner = call(
        first_level,
        [bf16(2, rows, half), bf16(2, rows, half), bf16(2, rows, half), f32(2, rows, half)],
        [square, square, squares, rim, rim],
        16,
        int(2.7e9),
        *owns,
        *mixes,
        keep,
        outer_got,
    )
    inner_other = exchange(inner, "cluster", 2)
    cross_far = exchange(cross, "tile", 2)
    summed = total_of(inner, inner_other)
    summed_far = exchange(summed, "tile", 2)
    cross_other = exchange(after(cross, summed), "cluster", 2)
    cross_far_other = exchange(cross_far, "cluster", 2)

    def with_core(x, y):
        return [x, y, exchange(x, "tile", 1), exchange(y, "tile", 1)]

    kept, sent, diagonal = call(
        last_level,
        [f32(2, few, nodes), bf16(2, few, nodes), f32(1, LANES)],
        [square, square, squares, pltpu.VMEM((2, rows, nodes), F32)],
        12,
        int(1.4e9),
        *with_core(summed, summed_far),
        *with_core(cross, cross_far),
        *with_core(cross_other, cross_far_other),
        left,
        corner,
        energy_weights,
        in_vmem=(12, 13),
        in_smem=(14,),
    )
    density = diagonal + exchange(diagonal, "cluster", 1)
    got_rows = exchange(sent, "cluster", 1).astype(F32)
    for distance in (1, 2):
        density = density + exchange(density, "energy", distance)
    density = jnp.where(side == 0, density[:, :few], density[:, few:])
    low = jnp.where(side == 0, kept, got_rows)
    high = jnp.where(side == 0, got_rows, kept)
    final_rows = jnp.stack([low, high]).transpose(2, 0, 1, 3)
    return final_rows[None], density


def solution(mesh):
    placed = (P("cluster", None, "tile", "energy", None, None), P("cluster", None), P("energy"))
    return jax.shard_map(
        compute,
        mesh=mesh,
        in_specs=placed,
        out_specs=(P("cluster", "tile", "energy", None, None), P("cluster", "tile")),
        check_vma=False,
    )
```

```python
import jax
import jax.numpy as jnp
from jax import lax
from jax.experimental import pallas as pl
from jax.experimental.pallas import tpu as pltpu
from jax.sharding import PartitionSpec as P


F32 = jnp.float32
BF16 = jnp.bfloat16
LANES = 128


def exchange(x, axis, distance):
    return lax.ppermute(x, axis, [(i, i ^ distance) for i in range(lax.axis_size(axis))])


def dot(x, y):
    return jnp.dot(x, y, preferred_element_type=F32)


def stacked(x):
    return x.reshape(2 * x.shape[1], x.shape[2])


def product(x, y_real, y_imag):
    rows = x.shape[0] // 2
    by_real, by_imag = dot(x, y_real), dot(x, y_imag)
    return by_real[:rows] - by_imag[rows:], by_imag[:rows] + by_real[rows:]


def halved(pair):
    return jnp.concatenate([pair[0].astype(BF16), pair[1].astype(BF16)], axis=0)


def at(start, size):
    return pl.ds(pl.multiple_of(start, size), size)


class Copies:
    def __init__(self, sems):
        self.sems = sems
        self.made = []

    def start(self, source, target):
        copy = pltpu.make_async_copy(source, target, self.sems.at[len(self.made)])
        copy.start()
        self.made.append(copy)
        return copy


def wait(copies):
    for copy in copies:
        copy.wait()


def call(body, out_shape, scratch, copies, flops, *args, in_vmem=(), in_smem=(), grant=40):
    spaces = [pltpu.HBM] * len(args)
    for i in in_vmem:
        spaces[i] = pltpu.VMEM
    for i in in_smem:
        spaces[i] = pltpu.SMEM
    return pl.pallas_call(
        body,
        out_shape=out_shape,
        in_specs=[pl.BlockSpec(memory_space=space) for space in spaces],
        out_specs=[pl.BlockSpec(memory_space=pltpu.VMEM)] * len(out_shape),
        scratch_shapes=scratch + [pltpu.SemaphoreType.DMA((copies,))],
        compiler_params=pltpu.CompilerParams(vmem_limit_bytes=grant << 20),
        cost_estimate=pl.CostEstimate(flops=flops, bytes_accessed=4 << 20, transcendentals=0),
    )(*args)


def places():
    cluster = lax.axis_index("cluster")
    tile = lax.axis_index("tile")
    return cluster % 2, tile // 2, tile % 2, cluster // 2 % 2


def fill_selector(column, selector):
    source = lax.broadcasted_iota(jnp.int32, selector.shape, 0)
    selector[...] = jnp.where(source == column, 1.0, 0.0).astype(BF16)


def reorder(stage, selector, parted):
    count, _, nodes = stage.shape
    flat = stage[...].reshape(2 * count, nodes)
    wide = 2 * LANES
    for first in range(0, selector.shape[1], wide):
        ordered = dot(flat, selector[:, first : first + wide])
        for turn in range(2):
            parted[first // LANES + turn] = ordered[:, turn * LANES : (turn + 1) * LANES]


def lane_block(parted, block, part, first, count):
    return parted[block, pl.ds(2 * first + part, count, stride=2), :].astype(BF16)


def order_cross(column_ref, raw, both_out, column, own_stage, other_stage, selector, parted, sems):
    side, _, _, _ = places()
    copies = Copies(sems)
    first = copies.start(column_ref, column)
    owned = copies.start(raw.at[0, 0, :, side], own_stage)
    other = copies.start(raw.at[0, 0, :, 1 - side], other_stage)
    first.wait()
    width = selector.shape[1]
    fill_selector(column[:, width:], selector)
    count = own_stage.shape[0]
    for turn, (copy, stage) in enumerate(((owned, own_stage), (other, other_stage))):
        copy.wait()
        reorder(stage, selector, parted.at[turn])
        for block in range(parted.shape[1]):
            first_lane = turn * width + block * LANES
            for part in range(2):
                both_out[part, :, first_lane : first_lane + LANES] = lane_block(
                    parted.at[turn], block, part, 0, count
                )


def order_first(
    column_ref, raw, send_out, inner_out,
    column, send_stage, own_stage, selector, send_parted, own_parted, sems,
):
    side, _, _, _ = places()
    copies = Copies(sems)
    first = copies.start(column_ref, column)
    sent = copies.start(raw.at[0, 0, :, 1 - side], send_stage)
    owned = copies.start(raw.at[0, 0, :, side], own_stage)
    first.wait()
    fill_selector(column[...], selector)
    sent.wait()
    reorder(send_stage, selector, send_parted)
    owned.wait()
    reorder(own_stage, selector.at[:, : inner_out.shape[2]], own_parted)
    count = send_stage.shape[0]
    for block in range(send_parted.shape[0]):
        lanes = slice(block * LANES, (block + 1) * LANES)
        for part in range(2):
            send_out[part, :, lanes] = lane_block(send_parted, block, part, 0, count)
            if lanes.stop <= inner_out.shape[2]:
                inner_out[part, :, lanes] = lane_block(own_parted, block, part, 0, count)


def order_second(
    column_ref, raw, send_out, keep_out,
    column, send_stage, own_stage, selector, send_parted, own_parted, sems,
):
    side, _, _, _ = places()
    copies = Copies(sems)
    first = copies.start(column_ref, column)
    sent = copies.start(raw.at[0, 1, :, 1 - side], send_stage)
    owned = copies.start(raw.at[0, 1, :, side], own_stage)
    first.wait()
    fill_selector(column[...], selector)
    sent.wait()
    reorder(send_stage, selector, send_parted)
    owned.wait()
    reorder(own_stage, selector, own_parted)
    count = send_stage.shape[0]
    for block in range(send_parted.shape[0]):
        lanes = slice(block * LANES, (block + 1) * LANES)
        for part in range(2):
            send_out[part, :, lanes] = lane_block(send_parted, block, part, 0, count)
            keep_out[part, :, lanes] = lane_block(own_parted, block, part, 0, count)


def guess(interior, approx):
    size = interior.shape[1]
    real = interior[0].astype(F32)
    imag = interior[1].astype(F32)

    def on_diagonal(count):
        return lax.broadcasted_iota(jnp.int32, (count, count), 0) == lax.broadcasted_iota(
            jnp.int32, (count, count), 1
        )

    block_diag = on_diagonal(LANES)

    def diagonal(values, axis):
        found = []
        for first in range(0, size, LANES):
            span = slice(first, first + LANES)
            block = jnp.where(block_diag, values[span, span], 0.0)
            found.append(jnp.sum(block, axis=axis, keepdims=True))
        return jnp.concatenate(found, axis=1 - axis)

    def reciprocal(axis):
        diag_real = diagonal(real, axis)
        diag_imag = diagonal(imag, axis)
        denom = diag_real * diag_real + diag_imag * diag_imag
        return diag_real / denom, -diag_imag / denom

    col_real, col_imag = reciprocal(0)
    row_real, row_imag = reciprocal(1)
    temp_real = real * col_real - imag * col_imag
    temp_imag = real * col_imag + imag * col_real
    prod_real = row_real * temp_real - row_imag * temp_imag
    prod_imag = row_real * temp_imag + row_imag * temp_real
    on_diag = on_diagonal(size)
    approx[0] = (jnp.where(on_diag, 2.0 * row_real, 0.0) - prod_real).astype(BF16)
    approx[1] = (jnp.where(on_diag, 2.0 * row_imag, 0.0) - prod_imag).astype(BF16)


def eliminate(left, interior, approx):
    applied = product(left, approx[0], approx[1])
    middle = halved(product(halved(applied), interior[0], interior[1]))
    second = product(middle, approx[0], approx[1])
    return halved((2.0 * applied[0] - second[0], 2.0 * applied[1] - second[1]))


def spread(copies, pieces, columns, target):
    _, depth, core, _ = places()
    rows = pieces[0].shape[1]
    made = []
    for who, piece in enumerate(pieces):
        row = at(((depth ^ (who % 2)) * 2 + (core ^ (who // 2))) * rows, rows)
        made.append(copies.start(piece.at[:, :, columns[who]], target.at[:, row]))
    return made


def first_level(*refs):
    sums, owns = refs[0:4], refs[4:8]
    others, keep, got = refs[8:12], refs[12], refs[13]
    inner_out, cross_out, left_out, corner_out = refs[14:18]
    interior, approx, right, left, start, sems = refs[18:]
    side, _, _, _ = places()
    copies = Copies(sems)
    width = interior.shape[1]
    rows = keep.shape[1]
    lows, highs = pl.ds(0, width), pl.ds(width, width)
    from_inner = spread(copies, sums, [lows] * 4, interior)
    from_outer = [
        copies.start(keep.at[:, :, lows], left.at[side]),
        copies.start(got.at[:, :, lows], left.at[1 - side]),
    ]
    from_cross = spread(copies, owns, [lows] * 4, right.at[side])
    from_cross += spread(copies, others, [highs, lows] * 2, right.at[1 - side])
    from_cross += [
        copies.start(keep.at[:, :, highs], start.at[side]),
        copies.start(got.at[:, :, highs], start.at[1 - side]),
    ]
    wait(from_inner)
    guess(interior, approx)
    wait(from_outer)
    both = jnp.concatenate([left[0, 0], left[1, 0], left[0, 1], left[1, 1]], axis=0)
    reduced = eliminate(both, interior, approx)
    wait(from_cross)
    low_taken = product(reduced, right[0, 0], right[0, 1])
    high_taken = product(reduced, right[1, 0], right[1, 1])
    for part in range(2):
        inner_out[part] = (start[0, part].astype(F32) - low_taken[part][:rows]).astype(BF16)
        cross_out[part] = (-high_taken[part][:rows]).astype(BF16)
        left_out[part] = (-low_taken[part][rows:]).astype(BF16)
        corner_out[part] = start[1, part].astype(F32) - high_taken[part][rows:]


def last_level(*refs):
    sums, owns, others = refs[0:4], refs[4:8], refs[8:12]
    left, corner, weights = refs[12:15]
    keep_out, send_out, diag_out = refs[15:18]
    interior, approx, right, total, sems = refs[18:]
    side, depth, core, pair = places()
    copies = Copies(sems)
    width = interior.shape[1]
    rows = corner.shape[1]
    few = rows // 2
    every = [pl.ds(0, width)] * 4
    from_inner = spread(copies, sums, every, interior)
    from_cross = spread(copies, owns, every, right.at[pair])
    from_cross += spread(copies, others, every, right.at[1 - pair])
    wait(from_inner)
    guess(interior, approx)
    reduced = eliminate(stacked(left[...]), interior, approx)
    wait(from_cross)
    for owner in range(2):
        taken = product(reduced, right[owner, 0], right[owner, 1])
        for part in range(2):
            start = jnp.where(pair == owner, corner[part], 0.0)
            total[part, :, owner * width : (owner + 1) * width] = start - taken[part]
    block = total[1, :, at(pair * width + (depth * 2 + core) * LANES, LANES)]
    row_of = lax.broadcasted_iota(jnp.int32, (rows, LANES), 0)
    lane_of = lax.broadcasted_iota(jnp.int32, (rows, LANES), 1)
    found = jnp.sum(jnp.where(row_of == lane_of, block, 0.0), axis=0, keepdims=True)
    diag_out[...] = found * weights[side]
    keep_rows, send_rows = at(side * few, few), at((1 - side) * few, few)
    for part in range(2):
        send_out[part] = total[part, send_rows, :].astype(BF16)
        keep_out[part] = total[part, keep_rows, :]


def finish(kept, got, out, sems):
    side, _, _, _ = places()
    for part in range(2):
        out[0, :, side, part, :] = kept[part]
        out[0, :, 1 - side, part, :] = got[part].astype(F32)


def after(x, *others):
    return lax.optimization_barrier((x,) + others)[0]


def compute(boundary, column_source, energy_weights):
    _, _, rows, _, _, nodes = boundary.shape
    half = nodes // 2
    few = rows // 2
    side = lax.axis_index("cluster") % 2

    def bf16(*shape):
        return jax.ShapeDtypeStruct(shape, BF16)

    def f32(*shape):
        return jax.ShapeDtypeStruct(shape, F32)

    def total_of(x, y):
        return (x.astype(F32) + y.astype(F32)).astype(BF16)

    selector = pltpu.VMEM((nodes, nodes), BF16)
    column = pltpu.VMEM((1, nodes), jnp.int32)
    stage = pltpu.VMEM((rows, 2, nodes), BF16)
    parted = pltpu.VMEM((nodes // LANES, 2 * rows, LANES), F32)
    ordering = [column, stage, stage, selector, parted, parted]
    (both,) = call(
        order_cross,
        [bf16(2, rows, nodes)],
        [
            column,
            stage,
            stage,
            pltpu.VMEM((nodes, half), BF16),
            pltpu.VMEM((2, half // LANES, 2 * rows, LANES), F32),
        ],
        3,
        int(1e9),
        column_source,
        boundary,
        grant=62,
    )
    both_far = exchange(both, "tile", 2)
    first, own_inner = call(
        order_first,
        [bf16(2, rows, nodes), bf16(2, rows, half)],
        ordering,
        3,
        int(2e9),
        after(column_source, both),
        boundary,
        grant=61,
    )
    got = exchange(first, "cluster", 1)
    outer, keep = call(
        order_second,
        [bf16(2, rows, nodes), bf16(2, rows, nodes)],
        ordering,
        3,
        int(2e9),
        after(column_source, own_inner),
        boundary,
        grant=40,
    )
    outer_got = exchange(after(outer, got), "cluster", 1)
    mixed = total_of(own_inner, got[..., :half])
    mixed_far = exchange(mixed, "tile", 2)
    both_far_other = exchange(both_far[..., half:], "cluster", 1)

    def with_core(x, y):
        return [x, y, exchange(x, "tile", 1), exchange(y, "tile", 1)]

    square = pltpu.VMEM((2, half, half), BF16)
    squares = pltpu.VMEM((2, 2, half, half), BF16)
    rim = pltpu.VMEM((2, 2, rows, half), BF16)
    inner, cross, left, corner = call(
        first_level,
        [bf16(2, rows, half), bf16(2, rows, half), bf16(2, rows, half), f32(2, rows, half)],
        [square, square, squares, rim, rim],
        16,
        int(2.7e9),
        *with_core(mixed, mixed_far),
        *with_core(both, both_far),
        *with_core(got, both_far_other),
        keep,
        outer_got,
    )
    inner_other = exchange(inner, "cluster", 2)
    cross_far = exchange(cross, "tile", 2)
    summed = total_of(inner, inner_other)
    summed_far = exchange(summed, "tile", 2)
    cross_other = exchange(after(cross, summed), "cluster", 2)
    cross_far_other = exchange(cross_far, "cluster", 2)

    kept, sent, diagonal = call(
        last_level,
        [f32(2, few, nodes), bf16(2, few, nodes), f32(1, LANES)],
        [square, square, squares, pltpu.VMEM((2, rows, nodes), F32)],
        12,
        int(1.4e9),
        *with_core(summed, summed_far),
        *with_core(cross, cross_far),
        *with_core(cross_other, cross_far_other),
        left,
        corner,
        energy_weights,
        in_vmem=(12, 13),
        in_smem=(14,),
    )
    density = diagonal + exchange(diagonal, "cluster", 1)
    got_rows = exchange(sent, "cluster", 1)
    parts = [exchange(density, "energy", distance) for distance in (1, 2, 3)]
    density = density + parts[0] + parts[1] + parts[2]
    density = jnp.where(side == 0, density[:, :few], density[:, few:])
    (final_rows,) = call(
        finish, [f32(1, few, 2, 2, nodes)], [], 1, int(1e6), kept, got_rows, in_vmem=(0, 1)
    )
    return final_rows, density


def solution(mesh):
    placed = (P("cluster", None, "tile", "energy", None, None), P("cluster", None), P("energy"))
    return jax.shard_map(
        compute,
        mesh=mesh,
        in_specs=placed,
        out_specs=(P("cluster", "tile", "energy", None, None), P("cluster", "tile")),
        check_vma=False,
    )
```

```python
import jax
import jax.numpy as jnp
from jax import lax
from jax.experimental import pallas as pl
from jax.experimental.pallas import tpu as pltpu
from jax.sharding import PartitionSpec as P


F32 = jnp.float32
BF16 = jnp.bfloat16
LANES = 128


def exchange(x, axis, distance):
    return lax.ppermute(x, axis, [(i, i ^ distance) for i in range(lax.axis_size(axis))])


def dot(x, y):
    return jnp.dot(x, y, preferred_element_type=F32)


def stacked(x):
    return x.reshape(2 * x.shape[1], x.shape[2])


def product(x, y_real, y_imag):
    rows = x.shape[0] // 2
    by_real, by_imag = dot(x, y_real), dot(x, y_imag)
    return by_real[:rows] - by_imag[rows:], by_imag[:rows] + by_real[rows:]


def halved(pair):
    return jnp.concatenate([pair[0].astype(BF16), pair[1].astype(BF16)], axis=0)


def at(start, size):
    return pl.ds(pl.multiple_of(start, size), size)


class Copies:
    def __init__(self, sems):
        self.sems = sems
        self.made = []

    def start(self, source, target):
        copy = pltpu.make_async_copy(source, target, self.sems.at[len(self.made)])
        copy.start()
        self.made.append(copy)
        return copy


def wait(copies):
    for copy in copies:
        copy.wait()


def call(body, out_shape, scratch, copies, flops, *args, in_vmem=(), in_smem=(), grant=40):
    spaces = [pltpu.HBM] * len(args)
    for i in in_vmem:
        spaces[i] = pltpu.VMEM
    for i in in_smem:
        spaces[i] = pltpu.SMEM
    return pl.pallas_call(
        body,
        out_shape=out_shape,
        in_specs=[pl.BlockSpec(memory_space=space) for space in spaces],
        out_specs=[pl.BlockSpec(memory_space=pltpu.VMEM)] * len(out_shape),
        scratch_shapes=scratch + [pltpu.SemaphoreType.DMA((copies,))],
        compiler_params=pltpu.CompilerParams(vmem_limit_bytes=grant << 20),
        cost_estimate=pl.CostEstimate(flops=flops, bytes_accessed=4 << 20, transcendentals=0),
    )(*args)


def places():
    cluster = lax.axis_index("cluster")
    tile = lax.axis_index("tile")
    return cluster % 2, tile // 2, tile % 2, cluster // 2 % 2


def fill_selector(column, selector):
    source = lax.broadcasted_iota(jnp.int32, selector.shape, 0)
    selector[...] = jnp.where(source == column, 1.0, 0.0).astype(BF16)


def reorder(stage, selector, parted):
    count, _, nodes = stage.shape
    flat = stage[...].reshape(2 * count, nodes)
    wide = 2 * LANES
    for first in range(0, selector.shape[1], wide):
        ordered = dot(flat, selector[:, first : first + wide])
        for turn in range(2):
            parted[first // LANES + turn] = ordered[:, turn * LANES : (turn + 1) * LANES]


def lane_block(parted, block, part, first, count):
    return parted[block, pl.ds(2 * first + part, count, stride=2), :].astype(BF16)


def order_cross(column_ref, raw, other_out, column, stage, selector, parted, sems):
    side, _, _, _ = places()
    copies = Copies(sems)
    first = copies.start(column_ref, column)
    other = copies.start(raw.at[0, 0, :, 1 - side], stage)
    first.wait()
    fill_selector(column[:, selector.shape[1] :], selector)
    other.wait()
    reorder(stage, selector, parted)
    for block in range(parted.shape[0]):
        for part in range(2):
            other_out[part, :, block * LANES : (block + 1) * LANES] = lane_block(
                parted, block, part, 0, stage.shape[0]
            )


def order_first(
    column_ref, raw, send_out, own_out,
    column, send_stage, own_stage, selector, send_parted, own_parted, sems,
):
    side, _, _, _ = places()
    copies = Copies(sems)
    first = copies.start(column_ref, column)
    sent = copies.start(raw.at[0, 0, :, 1 - side], send_stage)
    owned = copies.start(raw.at[0, 0, :, side], own_stage)
    first.wait()
    fill_selector(column[...], selector)
    sent.wait()
    reorder(send_stage, selector, send_parted)
    owned.wait()
    reorder(own_stage, selector.at[:, own_out.shape[2] :], own_parted)
    count = send_stage.shape[0]
    for block in range(send_parted.shape[0]):
        lanes = slice(block * LANES, (block + 1) * LANES)
        for part in range(2):
            send_out[part, :, lanes] = lane_block(send_parted, block, part, 0, count)
            if lanes.stop <= own_out.shape[2]:
                own_out[part, :, lanes] = lane_block(own_parted, block, part, 0, count)


def order_second(
    column_ref, raw, send_out, keep_out, inner_out,
    column, send_stage, own_stage, inner_stage, selector, send_parted, own_parted, inner_parted, sems,
):
    side, _, _, _ = places()
    copies = Copies(sems)
    first = copies.start(column_ref, column)
    inner = copies.start(raw.at[0, 0, :, side], inner_stage)
    sent = copies.start(raw.at[0, 1, :, 1 - side], send_stage)
    owned = copies.start(raw.at[0, 1, :, side], own_stage)
    first.wait()
    fill_selector(column[...], selector)
    inner.wait()
    width = inner_out.shape[2]
    reorder(inner_stage, selector.at[:, :width], inner_parted)
    sent.wait()
    reorder(send_stage, selector, send_parted)
    owned.wait()
    reorder(own_stage, selector, own_parted)
    count = send_stage.shape[0]
    for block in range(send_parted.shape[0]):
        lanes = slice(block * LANES, (block + 1) * LANES)
        for part in range(2):
            send_out[part, :, lanes] = lane_block(send_parted, block, part, 0, count)
            keep_out[part, :, lanes] = lane_block(own_parted, block, part, 0, count)
            if lanes.stop <= width:
                inner_out[part, :, lanes] = lane_block(inner_parted, block, part, 0, count)


def guess(interior, approx):
    size = interior.shape[1]
    real = interior[0].astype(F32)
    imag = interior[1].astype(F32)

    def on_diagonal(count):
        return lax.broadcasted_iota(jnp.int32, (count, count), 0) == lax.broadcasted_iota(
            jnp.int32, (count, count), 1
        )

    block_diag = on_diagonal(LANES)

    def diagonal(values, axis):
        found = []
        for first in range(0, size, LANES):
            span = slice(first, first + LANES)
            block = jnp.where(block_diag, values[span, span], 0.0)
            found.append(jnp.sum(block, axis=axis, keepdims=True))
        return jnp.concatenate(found, axis=1 - axis)

    def reciprocal(axis):
        diag_real = diagonal(real, axis)
        diag_imag = diagonal(imag, axis)
        denom = diag_real * diag_real + diag_imag * diag_imag
        return diag_real / denom, -diag_imag / denom

    col_real, col_imag = reciprocal(0)
    row_real, row_imag = reciprocal(1)
    temp_real = real * col_real - imag * col_imag
    temp_imag = real * col_imag + imag * col_real
    prod_real = row_real * temp_real - row_imag * temp_imag
    prod_imag = row_real * temp_imag + row_imag * temp_real
    on_diag = on_diagonal(size)
    approx[0] = (jnp.where(on_diag, 2.0 * row_real, 0.0) - prod_real).astype(BF16)
    approx[1] = (jnp.where(on_diag, 2.0 * row_imag, 0.0) - prod_imag).astype(BF16)


def eliminate(left, interior, approx):
    applied = product(left, approx[0], approx[1])
    middle = halved(product(halved(applied), interior[0], interior[1]))
    second = product(middle, approx[0], approx[1])
    return halved((2.0 * applied[0] - second[0], 2.0 * applied[1] - second[1]))


def spread(copies, pieces, columns, target):
    _, depth, core, _ = places()
    rows = pieces[0].shape[1]
    made = []
    for who, piece in enumerate(pieces):
        row = at(((depth ^ (who % 2)) * 2 + (core ^ (who // 2))) * rows, rows)
        made.append(copies.start(piece.at[:, :, columns[who]], target.at[:, row]))
    return made


def first_level(*refs):
    sums, owns = refs[0:4], refs[4:8]
    others, keep, got = refs[8:12], refs[12], refs[13]
    inner_out, cross_out, left_out, corner_out = refs[14:18]
    interior, approx, right, left, start, sems = refs[18:]
    side, _, _, _ = places()
    copies = Copies(sems)
    width = interior.shape[1]
    rows = keep.shape[1]
    lows, highs = pl.ds(0, width), pl.ds(width, width)
    from_inner = spread(copies, sums, [lows] * 4, interior)
    from_outer = [
        copies.start(keep.at[:, :, lows], left.at[side]),
        copies.start(got.at[:, :, lows], left.at[1 - side]),
    ]
    from_cross = spread(copies, owns, [lows] * 4, right.at[side])
    from_cross += spread(copies, others, [highs, lows] * 2, right.at[1 - side])
    from_cross += [
        copies.start(keep.at[:, :, highs], start.at[side]),
        copies.start(got.at[:, :, highs], start.at[1 - side]),
    ]
    wait(from_inner)
    guess(interior, approx)
    wait(from_outer)
    both = jnp.concatenate([left[0, 0], left[1, 0], left[0, 1], left[1, 1]], axis=0)
    reduced = eliminate(both, interior, approx)
    wait(from_cross)
    low_taken = product(reduced, right[0, 0], right[0, 1])
    high_taken = product(reduced, right[1, 0], right[1, 1])
    for part in range(2):
        inner_out[part] = (start[0, part].astype(F32) - low_taken[part][:rows]).astype(BF16)
        cross_out[part] = (-high_taken[part][:rows]).astype(BF16)
        left_out[part] = (-low_taken[part][rows:]).astype(BF16)
        corner_out[part] = start[1, part].astype(F32) - high_taken[part][rows:]


def last_level(*refs):
    sums, owns, others = refs[0:4], refs[4:8], refs[8:12]
    left, corner, weights = refs[12:15]
    keep_out, send_out, diag_out = refs[15:18]
    interior, approx, right, total, sems = refs[18:]
    side, depth, core, pair = places()
    copies = Copies(sems)
    width = interior.shape[1]
    rows = corner.shape[1]
    few = rows // 2
    every = [pl.ds(0, width)] * 4
    from_inner = spread(copies, sums, every, interior)
    from_cross = spread(copies, owns, every, right.at[pair])
    from_cross += spread(copies, others, every, right.at[1 - pair])
    wait(from_inner)
    guess(interior, approx)
    reduced = eliminate(stacked(left[...]), interior, approx)
    wait(from_cross)
    for owner in range(2):
        taken = product(reduced, right[owner, 0], right[owner, 1])
        for part in range(2):
            start = jnp.where(pair == owner, corner[part], 0.0)
            total[part, :, owner * width : (owner + 1) * width] = start - taken[part]
    block = total[1, :, at(pair * width + (depth * 2 + core) * LANES, LANES)]
    row_of = lax.broadcasted_iota(jnp.int32, (rows, LANES), 0)
    lane_of = lax.broadcasted_iota(jnp.int32, (rows, LANES), 1)
    found = jnp.sum(jnp.where(row_of == lane_of, block, 0.0), axis=0, keepdims=True)
    diag_out[...] = found * weights[side]
    keep_rows, send_rows = at(side * few, few), at((1 - side) * few, few)
    for part in range(2):
        send_out[part] = total[part, send_rows, :].astype(BF16)
        keep_out[part] = total[part, keep_rows, :]


def finish(kept, got, out, sems):
    side, _, _, _ = places()
    for part in range(2):
        out[0, :, side, part, :] = kept[part]
        out[0, :, 1 - side, part, :] = got[part].astype(F32)


def after(x, *others):
    return lax.optimization_barrier((x,) + others)[0]


def compute(boundary, column_source, energy_weights):
    _, _, rows, _, _, nodes = boundary.shape
    half = nodes // 2
    few = rows // 2
    side = lax.axis_index("cluster") % 2

    def bf16(*shape):
        return jax.ShapeDtypeStruct(shape, BF16)

    def f32(*shape):
        return jax.ShapeDtypeStruct(shape, F32)

    def total_of(x, y):
        return (x.astype(F32) + y.astype(F32)).astype(BF16)

    selector = pltpu.VMEM((nodes, nodes), BF16)
    column = pltpu.VMEM((1, nodes), jnp.int32)
    stage = pltpu.VMEM((rows, 2, nodes), BF16)
    parted = pltpu.VMEM((nodes // LANES, 2 * rows, LANES), F32)
    (other,) = call(
        order_cross,
        [bf16(2, rows, half)],
        [
            column,
            stage,
            pltpu.VMEM((nodes, half), BF16),
            pltpu.VMEM((half // LANES, 2 * rows, LANES), F32),
        ],
        2,
        int(1e9),
        column_source,
        boundary,
        grant=62,
    )
    other_far = exchange(other, "tile", 2)
    first, own = call(
        order_first,
        [bf16(2, rows, nodes), bf16(2, rows, half)],
        [column, stage, stage, selector, parted, parted],
        3,
        int(2e9),
        after(column_source, other),
        boundary,
        grant=61,
    )
    own_far = exchange(own, "tile", 2)
    got = exchange(first, "cluster", 1)
    outer, keep, own_inner = call(
        order_second,
        [bf16(2, rows, nodes), bf16(2, rows, nodes), bf16(2, rows, half)],
        [column, stage, stage, stage, selector, parted, parted, parted],
        4,
        int(3e9),
        after(column_source, first),
        boundary,
    )
    outer_got = exchange(after(outer, got), "cluster", 1)
    mixed = total_of(own_inner, got[..., :half])
    mixed_far = exchange(mixed, "tile", 2)
    sibling_far = exchange(other_far, "cluster", 1)

    def with_core(x, y):
        return [x, y, exchange(x, "tile", 1), exchange(y, "tile", 1)]

    square = pltpu.VMEM((2, half, half), BF16)
    squares = pltpu.VMEM((2, 2, half, half), BF16)
    rim = pltpu.VMEM((2, 2, rows, half), BF16)
    inner, cross, left, corner = call(
        first_level,
        [bf16(2, rows, half), bf16(2, rows, half), bf16(2, rows, half), f32(2, rows, half)],
        [square, square, squares, rim, rim],
        16,
        int(2.7e9),
        *with_core(mixed, mixed_far),
        *with_core(own, own_far),
        *with_core(got, sibling_far),
        keep,
        outer_got,
    )
    inner_other = exchange(inner, "cluster", 2)
    cross_far = exchange(cross, "tile", 2)
    summed = total_of(inner, inner_other)
    summed_far = exchange(summed, "tile", 2)
    cross_other = exchange(after(cross, summed), "cluster", 2)
    cross_far_other = exchange(cross_far, "cluster", 2)

    kept, sent, diagonal = call(
        last_level,
        [f32(2, few, nodes), bf16(2, few, nodes), f32(1, LANES)],
        [square, square, squares, pltpu.VMEM((2, rows, nodes), F32)],
        12,
        int(1.4e9),
        *with_core(summed, summed_far),
        *with_core(cross, cross_far),
        *with_core(cross_other, cross_far_other),
        left,
        corner,
        energy_weights,
        in_vmem=(12, 13),
        in_smem=(14,),
    )
    density = diagonal + exchange(diagonal, "cluster", 1)
    got_rows = exchange(sent, "cluster", 1)
    parts = [exchange(density, "energy", distance) for distance in (1, 2, 3)]
    density = density + parts[0] + parts[1] + parts[2]
    density = jnp.where(side == 0, density[:, :few], density[:, few:])
    (final_rows,) = call(
        finish, [f32(1, few, 2, 2, nodes)], [], 1, int(1e6), kept, got_rows, in_vmem=(0, 1)
    )
    return final_rows, density


def solution(mesh):
    placed = (P("cluster", None, "tile", "energy", None, None), P("cluster", None), P("energy"))
    return jax.shard_map(
        compute,
        mesh=mesh,
        in_specs=placed,
        out_specs=(P("cluster", "tile", "energy", None, None), P("cluster", "tile")),
        check_vma=False,
    )
```
